32 devices in a mesh: ckpt: 8 (over y, x, core), vocab: 4 (over z).
Axes of the slice: x: 2, y: 2, z: 4, core: 2. Of those that a mesh axis runs over, the one named last changes fastest.
Arguments:
- hidden_rows: bfloat16 [8, 128, 768], P('ckpt'), may hold values from -8 to 8
- norm_gain: float32 [8, 768], P('ckpt'), may hold values from 0.5 to 1.5
- norm_bias: float32 [8, 768], P('ckpt'), may hold values from -1.2 to 1.2
- unembed: bfloat16 [8, 768, 50304], P('ckpt', None, 'vocab'), may hold values from -6 to 6
- target_ids: int32 [128], replicated, may hold values from 0 to 50303
- ckpt_steps: int32 [8], replicated, may hold values from 0 to 143000
- components: int32 [1], replicated, may hold values from 1 to 8
Outputs:
- loadings: bfloat16 [8, 128, 50304], P(None, 'ckpt', 'vocab')
- gram: float32 [8, 8], replicated
- target_logprob: float32 [8, 128], P('ckpt')
The draws below stay inside these ranges and needn't reach their ends.
All inputs are finite; a program needn't handle non-finite values.
Results may differ from the reference program's by a relative error of at most 0.0063.
Values may be sent and summed in bfloat16 or wider, within the bound.
A program may use at most 192 MiB of HBM per device.

```python
import jax
import jax.numpy as jnp
from jax import lax

D = 768
V = 50304
TOK_SLAB = 16
COMPONENTS = 8
CKPTS = 8
TOKENS = 128
N_CKPT = 8


def unit_draw(key, shape):
    return jax.random.normal(key, shape, jnp.float32)


def mixture():
    return (0.8, 0.45, 0.4)


def drift_weights(key, directions):
    increments = jax.random.normal(key, (CKPTS, directions), jnp.float32)
    walk = jnp.cumsum(increments, axis=0)
    walk = walk - jnp.mean(walk, axis=0, keepdims=True)
    spread = jnp.sqrt(jnp.mean(walk * walk, axis=0, keepdims=True))
    return walk / (spread + 0.001)


def column_boost(key):
    length = max(V // 192, 1)
    starts = jax.random.randint(jax.random.fold_in(key, 27), (8,), 0, V - length + 1)
    strength = jnp.exp(jax.random.uniform(jax.random.fold_in(key, 28), (8,), jnp.float32, 0.693, 1.609))
    positions = jnp.arange(V, dtype=jnp.int32)
    inside = (positions[None, :] >= starts[:, None]) & (positions[None, :] < starts[:, None] + length)
    return jnp.max(jnp.where(inside, strength[:, None], 1.0), axis=0)


def base_hidden(key):
    shared_part, drift_part, noise_part = mixture()
    shared = unit_draw(jax.random.fold_in(key, 11), (TOKENS, D))
    paths = unit_draw(jax.random.fold_in(key, 13), (4, TOKENS, D))
    weights = drift_weights(jax.random.fold_in(key, 14), 4)
    drift = jnp.einsum('cj,jtd->ctd', weights, paths) / 2.0
    noise = unit_draw(jax.random.fold_in(key, 15), (CKPTS, TOKENS, D))
    values = shared_part * shared[None, :, :] + drift_part * drift + noise_part * noise
    return jnp.clip(values, -8.0, 8.0)


def draw_hidden_rows(key, part):
    return base_hidden(key).astype(jnp.bfloat16)


def draw_unembed(key, part):
    scale = 3.0 / jnp.sqrt(jnp.float32(D))
    bound = 4.0 + 2000 // D
    shared_part, drift_part, noise_part = mixture()
    shared = unit_draw(jax.random.fold_in(key, 21), (D, V))
    paths = unit_draw(jax.random.fold_in(key, 24), (4, D, V))
    weights = drift_weights(jax.random.fold_in(key, 25), 4)
    boost = column_boost(key)
    noise_key = jax.random.fold_in(key, 26)

    def one_ckpt(index):
        noise = unit_draw(jax.random.fold_in(noise_key, index), (D, V))
        drift = jnp.tensordot(weights[index], paths, axes=1) / 2.0 * boost[None, :]
        matrix = (shared_part * shared + drift_part * drift + noise_part * noise) * scale
        return jnp.clip(matrix, -bound, bound).astype(jnp.bfloat16)
    return lax.map(one_ckpt, jnp.arange(CKPTS, dtype=jnp.int32))


def with_ends(drawn, stream_key, smallest, high):
    longest = drawn.shape.index(max(drawn.shape))
    spots = []
    for shift in (0, 1):
        where = [jax.random.randint(jax.random.fold_in(stream_key, axis), (), 0, length) for axis, length in enumerate(drawn.shape)]
        where[longest] = (where[longest] + shift) % drawn.shape[longest]
        spots.append(tuple(where))
    return drawn.at[spots[0]].set(smallest).at[spots[1]].set(high)


def shard_levels(own_key, extent, shards, low, top_value):
    def one(position, shards_of):
        draws = jax.random.uniform(jax.random.fold_in(jax.random.fold_in(own_key, 6), position), (shards_of,), jnp.float32, low / len(shards), top_value / len(shards))
        return jnp.repeat(jnp.exp(draws), extent[position] // shards_of).reshape((-1,) + (1,) * (len(extent) - position - 1))

    factor_of = one(*shards[0])
    for cut in shards[1:]:
        factor_of = factor_of * one(*cut)
    return factor_of


def bell_draw(own_key, dims, scale, reach, cuts=(), held_as=jnp.bfloat16):
    level = shard_levels(own_key, dims, cuts, -0.22, 0.18) if cuts else 1.0
    drawn = jax.random.normal(own_key, dims, jnp.float32) * scale * level
    return jnp.minimum(jnp.maximum(drawn, -reach), reach).astype(held_as)


def setup_inputs(seed: int = 0) -> dict:
    key_list = jax.random.split(jax.random.key(seed), 8)
    return {
        "hidden_rows": draw_hidden_rows(jax.random.fold_in(key_list[7], 71), 0),
        "norm_gain": jnp.clip(1.0 + 0.1 * jax.random.normal(key_list[1], (CKPTS, D), jnp.float32), 0.5, 1.5),
        "norm_bias": bell_draw(key_list[2], (CKPTS, D), 0.2, 1.2, ((0, 8),), jnp.float32),
        "unembed": draw_unembed(jax.random.fold_in(key_list[7], 71), 0),
        "target_ids": with_ends(jax.random.randint(key_list[4], (TOKENS,), 0, V), jax.random.fold_in(key_list[4], 1), 0, V - 1).astype(jnp.int32),
        "ckpt_steps": with_ends(jax.random.randint(key_list[5], (CKPTS,), 0, 143001), jax.random.fold_in(key_list[5], 1), 0, 143000).astype(jnp.int32),
        "components": jax.random.randint(key_list[6], (1,), 1, COMPONENTS + 1).astype(jnp.int32),
    }


def one_checkpoint(items, target_ids):
    rows, gain, bias, weights = items
    floats = rows.astype(jnp.float32)
    centre = lax.optimization_barrier(jnp.mean(floats, axis=1, keepdims=True))
    spread = lax.optimization_barrier(jnp.mean((floats - centre) ** 2, axis=1, keepdims=True))
    normed = ((floats - centre) / jnp.sqrt(spread + 1e-05) * gain[None, :] + bias[None, :]).astype(jnp.bfloat16)
    logits = jnp.dot(normed, weights, preferred_element_type=jnp.float32)
    top = lax.optimization_barrier(jnp.max(logits, axis=1, keepdims=True))
    lse = top + jnp.log(lax.optimization_barrier(jnp.sum(jnp.exp(logits - top), axis=1, keepdims=True)))
    logprob = (logits - lse).astype(jnp.bfloat16)
    picked = jnp.take_along_axis(logits, target_ids[:, None].astype(jnp.int32), axis=1)
    return (logprob, (picked - lse)[:, 0])

def slab_centred(logprob_all, index):
    piece = lax.dynamic_slice_in_dim(logprob_all, (index * TOK_SLAB).astype(jnp.int32), TOK_SLAB, 1)
    floats = piece.astype(jnp.float32)
    return floats - lax.optimization_barrier(jnp.mean(floats, axis=0, keepdims=True))

def reference(hidden_rows, norm_gain, norm_bias, unembed, target_ids, ckpt_steps, components):
    logprob_all, target_logprob = lax.map(lambda items: one_checkpoint(items, target_ids), (hidden_rows, norm_gain, norm_bias, unembed))
    slab_index = jnp.arange(N_CKPT, dtype=jnp.int32)

    def add_slab(total, index):
        centred = slab_centred(logprob_all, index)
        part = jnp.einsum('ctv,dtv->cd', centred, centred, precision=lax.Precision.HIGHEST)
        return (total + part, None)
    total, unused = lax.scan(add_slab, jnp.zeros((CKPTS, CKPTS), jnp.float32), slab_index)
    gram = total / (TOKENS * V)
    freqs = jnp.arange(COMPONENTS).astype(jnp.float32) + 1.0
    basis = jnp.cos(jnp.pi * freqs[None, :] * ckpt_steps.astype(jnp.float32)[:, None] / 143000.0)
    trace = jnp.sum(jnp.diagonal(gram))
    mixing = jnp.dot(gram, basis, precision=lax.Precision.HIGHEST) / (trace / CKPTS + 1e-06)
    keep = (jnp.arange(COMPONENTS) < components[0]).astype(jnp.float32)

    def slab_loadings(index):
        centred = slab_centred(logprob_all, index)
        mixed = jnp.einsum('ctv,ck->ktv', centred, mixing, precision=lax.Precision.HIGHEST) / CKPTS
        return (mixed * keep[:, None, None]).astype(jnp.bfloat16)
    pieces = lax.map(slab_loadings, slab_index)
    loadings = jnp.transpose(pieces, (1, 0, 2, 3)).reshape(COMPONENTS, TOKENS, V)
    return (loadings, gram, target_logprob)
```

```python
import functools

import jax
import jax.numpy as jnp
from jax import lax
from jax.experimental import pallas as pl
from jax.experimental.pallas import tpu as pltpu
from jax.sharding import PartitionSpec as P

COMPONENTS = 8
LANES = 128
HIGH = lax.Precision.HIGHEST
MESH = pl.DeviceIdType.MESH
LOW = -1e30
NT = (((1,), (1,)), ((), ()))


def split_tiles(width):
    tiles = -(-width // LANES)
    best = tiles
    for per in range(1, tiles + 1):
        if tiles % per == 0 and per >= 6:
            best = per
            break
    return best * LANES, tiles // best


def spread_steps(steps_ref, shape, slab):
    lane_owner = lax.broadcasted_iota(jnp.int32, shape, 1) // slab
    out = jnp.zeros(shape, jnp.float32)
    for c in range(steps_ref.shape[0]):
        out = jnp.where(lane_owner == c, steps_ref[c].astype(jnp.float32), out)
    return out


def gather_kernel(
    sizes,
    hidden_ref, gain_ref, bias_ref, ids_ref, steps_ref, comps_ref, w_ref,
    xout_ref, whi_ref, wlo_ref, shift_ref, gram_ref, target_ref,
    normed, xsend, xrecv, off, ids, tops, sums, hits, stat, stats, dsend, drecv,
    gsend, grecv, hsend, hrecv,
    send_sem, recv_sem, out_sem, ssend, srecv, dssem, drsem, gssem, grsem, hssem, hrsem,
):
    owners, shards, tokens, width, tile, chunks = sizes
    slab = tokens // owners
    rows = owners * slab
    kinds = COMPONENTS
    me = lax.axis_index("ckpt")
    mine = lax.axis_index("vocab")
    step = pl.program_id(0)
    groups = tile // LANES
    my_rows = pl.ds(pl.multiple_of(me * slab, slab), slab)

    def peer(r):
        return lax.rem(me + r, owners)

    def side(r):
        return lax.rem(mine + r, shards)

    @pl.when(step == 0)
    def _():
        barrier = pltpu.get_barrier_semaphore()
        for r in range(1, owners):
            pl.semaphore_signal(barrier, inc=1, device_id=(peer(r), mine), device_id_type=MESH)
        for r in range(1, shards):
            pl.semaphore_signal(barrier, inc=1, device_id=(me, side(r)), device_id_type=MESH)
        floats = hidden_ref[...].astype(jnp.float32)
        centre = jnp.mean(floats, axis=1, keepdims=True)
        spread = jnp.mean((floats - centre) ** 2, axis=1, keepdims=True)
        normed[...] = (
            (floats - centre) / jnp.sqrt(spread + 1e-05) * gain_ref[...] + bias_ref[...]
        ).astype(jnp.bfloat16)
        wide = jnp.broadcast_to(ids_ref[...].astype(jnp.float32), (LANES, tokens))
        ids[...] = jnp.transpose(wide).astype(jnp.int32)
        tops[...] = jnp.full_like(tops, LOW)
        sums[...] = jnp.zeros_like(sums)
        hits[...] = jnp.zeros_like(hits)

    logits = jnp.dot(normed[...], w_ref[...], preferred_element_type=jnp.float32)
    first = step * tile
    lane = lax.broadcasted_iota(jnp.int32, (tokens, LANES), 1)

    @pl.when(step == 0)
    def _():
        total = logits[:, :LANES]
        for g in range(1, groups):
            total = total + logits[:, g * LANES:(g + 1) * LANES]
        off[...] = jnp.broadcast_to(
            jnp.sum(total, axis=1, keepdims=True) * (1.0 / tile), off.shape
        )

    shift = off[...]
    for g in range(groups):
        part = logits[:, g * LANES:(g + 1) * LANES]
        inside = (first + g * LANES + lane) < width
        at = pl.multiple_of(first + g * LANES, LANES)
        xsend[:, pl.ds(at, LANES)] = jnp.where(inside, part - shift, 0.0).astype(jnp.bfloat16)

    @pl.when(step == 0)
    def _():
        barrier = pltpu.get_barrier_semaphore()
        pl.semaphore_wait(barrier, owners - 1 + shards - 1)

    def columns(j):
        return pl.ds(pl.multiple_of(j * tile, LANES), tile)

    for r in range(1, owners):
        to = peer(r)
        pltpu.make_async_remote_copy(
            src_ref=xsend.at[pl.ds(pl.multiple_of(to * slab, slab), slab), columns(step)],
            dst_ref=xrecv.at[my_rows, columns(step)],
            send_sem=send_sem.at[r],
            recv_sem=recv_sem.at[step],
            device_id=(to, mine),
            device_id_type=MESH,
        ).start()
    pltpu.make_async_copy(
        xsend.at[my_rows, columns(step)], xrecv.at[my_rows, columns(step)], recv_sem.at[step]
    ).start()

    old_top = tops[...]
    new_top = old_top
    parts = []
    for g in range(groups):
        part = logits[:, g * LANES:(g + 1) * LANES]
        inside = (first + g * LANES + lane) < width
        part = jnp.where(inside, part, LOW)
        parts.append(part)
        new_top = jnp.maximum(new_top, part)
    acc = sums[...] * jnp.exp(old_top - new_top)
    hit = hits[...]
    start = mine * width + first
    wanted = ids[...] - start
    for g in range(groups):
        acc = acc + jnp.exp(parts[g] - new_top)
        col = g * LANES + lane
        hit = hit + jnp.where((col == wanted) & ((first + col) < width), parts[g], 0.0)
    tops[...] = new_top
    sums[...] = acc
    hits[...] = hit

    @pl.when(step == chunks - 1)
    def _():
        top = jnp.max(tops[...], axis=1, keepdims=True)
        total = jnp.sum(sums[...] * jnp.exp(tops[...] - top), axis=1, keepdims=True)
        picked = jnp.sum(hits[...], axis=1, keepdims=True)
        stat[...] = jnp.where(lane == 0, top, jnp.where(lane == 1, total, picked))
        sent = []
        for r in range(1, shards):
            copy = pltpu.make_async_remote_copy(
                src_ref=stat,
                dst_ref=stats.at[r - 1],
                send_sem=ssend.at[r - 1],
                recv_sem=srecv.at[r - 1],
                device_id=(me, side(r)),
                device_id_type=MESH,
            )
            copy.start()
            sent.append(copy)
        for copy in sent:
            copy.wait()
        best = top
        for r in range(shards - 1):
            best = jnp.maximum(best, stats[r][:, 0:1])
        total = total * jnp.exp(top - best)
        for r in range(shards - 1):
            total = total + stats[r][:, 1:2] * jnp.exp(stats[r][:, 0:1] - best)
            picked = picked + stats[r][:, 2:3]
        lse = best + jnp.log(total)
        dsend[...] = jnp.broadcast_to(off[:, 0:1] - lse, dsend.shape)
        dcopies = []
        for r in range(1, owners):
            to = peer(r)
            copy = pltpu.make_async_remote_copy(
                src_ref=dsend.at[pl.ds(pl.multiple_of(to * slab, slab), slab), :],
                dst_ref=drecv.at[my_rows, :],
                send_sem=dssem.at[0],
                recv_sem=drsem.at[0],
                device_id=(to, mine),
                device_id_type=MESH,
            )
            copy.start()
        pltpu.make_async_copy(dsend.at[my_rows, :], drecv.at[my_rows, :], drsem.at[0]).start()
        target_ref[...] = jnp.transpose(
            jnp.broadcast_to(picked - lse, (tokens, LANES))
        )[0:1, :]

        row_k = lax.broadcasted_iota(jnp.int32, (kinds * slab, rows), 0)
        freqs = (row_k // slab + 1).astype(jnp.float32)
        at_steps = spread_steps(steps_ref, (kinds * slab, rows), slab)
        basis = jnp.cos(jnp.pi * freqs * at_steps / 143000.0)
        basis = basis - jnp.mean(basis, axis=1, keepdims=True)
        same = (row_k % slab) == (lax.broadcasted_iota(jnp.int32, (kinds * slab, rows), 1) % slab)
        keep = same & (row_k // slab < comps_ref[0])
        ones = jnp.ones((tile, LANES), jnp.bfloat16)

        def absorb(j, carry):
            products, totals = carry
            block = xrecv.at[:, columns(j)]
            pltpu.make_async_copy(block, block, recv_sem.at[j]).wait()
            pltpu.make_async_copy(block, xout_ref.at[:, columns(j)], out_sem.at[0]).start()
            x = block[...]
            products = products + lax.dot_general(x, x, NT, preferred_element_type=jnp.float32)
            totals = totals + jnp.dot(x, ones, preferred_element_type=jnp.float32)
            return products, totals

        products, totals = lax.fori_loop(
            0, chunks, absorb,
            (jnp.zeros((rows, rows), jnp.float32), jnp.zeros((rows, LANES), jnp.float32)),
        )
        pltpu.make_async_copy(drecv, drecv, drsem.at[0]).wait()
        d = drecv[...].reshape(owners, slab, LANES)
        d = (d - jnp.mean(d, axis=0, keepdims=True)).reshape(rows, LANES)
        lane_r = lax.broadcasted_iota(jnp.int32, (rows, LANES), 1)
        left = jnp.where(lane_r == 0, totals, jnp.where(lane_r == 1, d, 0.0))
        right = jnp.where(
            lane_r == 0, d, jnp.where(lane_r == 1, totals + float(width) * d, 0.0)
        )
        products = products + lax.dot_general(
            left, right, NT, precision=HIGH, preferred_element_type=jnp.float32
        )
        matched = (
            lax.broadcasted_iota(jnp.int32, (rows, rows), 0) % slab
            == lax.broadcasted_iota(jnp.int32, (rows, rows), 1) % slab
        )
        partial = jnp.sum(
            jnp.where(matched, products, 0.0).reshape(owners, slab, rows), axis=1
        )
        gsend[...] = partial
        gcopies = []
        for r in range(1, owners):
            copy = pltpu.make_async_remote_copy(
                src_ref=gsend,
                dst_ref=grecv.at[me],
                send_sem=gssem.at[0],
                recv_sem=grsem.at[0],
                device_id=(peer(r), mine),
                device_id_type=MESH,
            )
            copy.start()
        pltpu.make_async_copy(gsend, grecv.at[me], grsem.at[0]).start()
        pltpu.make_async_copy(grecv, grecv, grsem.at[0]).wait()
        hsend[...] = jnp.sum(grecv[...], axis=0)
        for r in range(1, shards):
            pltpu.make_async_remote_copy(
                src_ref=hsend,
                dst_ref=hrecv.at[mine],
                send_sem=hssem.at[0],
                recv_sem=hrsem.at[0],
                device_id=(me, side(r)),
                device_id_type=MESH,
            ).start()
        pltpu.make_async_copy(hsend, hrecv.at[mine], hrsem.at[0]).start()
        pltpu.make_async_copy(hrecv, hrecv, hrsem.at[0]).wait()
        full = jnp.sum(hrecv[...], axis=0) * (1.0 / (tokens * width * shards))
        full = full - jnp.mean(full, axis=0, keepdims=True)
        own = (
            lax.broadcasted_iota(jnp.int32, (owners, rows), 0)
            == lax.broadcasted_iota(jnp.int32, (owners, rows), 1) // slab
        )
        trace = jnp.sum(
            jnp.sum(jnp.where(own, full, 0.0), axis=1, keepdims=True), axis=0, keepdims=True
        )
        tall = jnp.broadcast_to(full[:, None, :], (owners, slab, rows)).reshape(rows, rows)
        mixed = lax.dot_general(
            basis, tall, NT, precision=HIGH, preferred_element_type=jnp.float32
        )
        mixed = jnp.where(keep, mixed / (trace * (1.0 / owners) + 1e-06) * (1.0 / owners), 0.0)
        high = mixed.astype(jnp.bfloat16)
        whi_ref[...] = high
        wlo_ref[...] = (mixed - high.astype(jnp.float32)).astype(jnp.bfloat16)
        shift_ref[...] = jnp.dot(mixed, d, precision=HIGH, preferred_element_type=jnp.float32)
        pick = (
            lax.broadcasted_iota(jnp.int32, (rows, LANES), 0) // slab
            == lax.broadcasted_iota(jnp.int32, (rows, LANES), 1)
        ).astype(jnp.float32) - 1.0 / owners
        gram_ref[...] = jnp.dot(
            full, pick, precision=HIGH, preferred_element_type=jnp.float32
        )[:, :owners]

        for r in range(1, owners):
            strip = xsend.at[my_rows, :]
            pltpu.make_async_copy(strip, strip, send_sem.at[r]).wait()
        others = pl.ds(0, rows - slab)
        pltpu.make_async_copy(dsend.at[others, :], dsend.at[others, :], dssem.at[0]).wait()
        less = pl.ds(0, owners - 1)
        pltpu.make_async_copy(grecv.at[less], grecv.at[less], gssem.at[0]).wait()
        fewer = pl.ds(0, shards - 1)
        pltpu.make_async_copy(hrecv.at[fewer], hrecv.at[fewer], hssem.at[0]).wait()
        pltpu.make_async_copy(xrecv, xout_ref, out_sem.at[0]).wait()


def mix_kernel(x_ref, whi_ref, wlo_ref, shift_ref, gram_in, target_in, out_ref, gram_ref, target_ref):
    x = x_ref[...]
    mixed = jnp.dot(whi_ref[...], x, preferred_element_type=jnp.float32)
    mixed = mixed + jnp.dot(wlo_ref[...], x, preferred_element_type=jnp.float32)
    out_ref[...] = (mixed + shift_ref[:, 0:1]).astype(jnp.bfloat16)
    gram_ref[...] = gram_in[...]
    target_ref[...] = target_in[...]


def per_device(owners, shards, hidden_rows, norm_gain, norm_bias, unembed, target_ids, ckpt_steps, components):
    tokens, depth = hidden_rows.shape[1:]
    width = unembed.shape[2]
    slab = tokens // owners
    rows = owners * slab
    out_rows = COMPONENTS * slab
    tile, chunks = split_tiles(width)
    padded = tile * chunks
    sizes = (owners, shards, tokens, width, tile, chunks)
    f32, bf16 = jnp.float32, jnp.bfloat16
    vmem = pl.BlockSpec(memory_space=pltpu.VMEM)
    smem = pl.BlockSpec(memory_space=pltpu.SMEM)
    dma = pltpu.SemaphoreType.DMA

    x, whi, wlo, shift, gram, target = pl.pallas_call(
        functools.partial(gather_kernel, sizes),
        grid=(chunks,),
        in_specs=[
            vmem, vmem, vmem, vmem, smem, smem,
            pl.BlockSpec((depth, tile), lambda j: (0, j)),
        ],
        out_specs=[pl.BlockSpec(memory_space=pl.ANY), vmem, vmem, vmem, vmem, vmem],
        out_shape=[
            jax.ShapeDtypeStruct((rows, padded), bf16),
            jax.ShapeDtypeStruct((out_rows, rows), bf16),
            jax.ShapeDtypeStruct((out_rows, rows), bf16),
            jax.ShapeDtypeStruct((out_rows, LANES), f32),
            jax.ShapeDtypeStruct((owners, owners), f32),
            jax.ShapeDtypeStruct((1, tokens), f32),
        ],
        scratch_shapes=[
            pltpu.VMEM((tokens, depth), bf16),
            pltpu.VMEM((tokens, padded), bf16),
            pltpu.VMEM((rows, padded), bf16),
            pltpu.VMEM((tokens, LANES), f32),
            pltpu.VMEM((tokens, LANES), jnp.int32),
            pltpu.VMEM((tokens, LANES), f32),
            pltpu.VMEM((tokens, LANES), f32),
            pltpu.VMEM((tokens, LANES), f32),
            pltpu.VMEM((tokens, LANES), f32),
            pltpu.VMEM((shards - 1, tokens, LANES), f32),
            pltpu.VMEM((tokens, LANES), f32),
            pltpu.VMEM((rows, LANES), f32),
            pltpu.VMEM((owners, rows), f32),
            pltpu.VMEM((owners, owners, rows), f32),
            pltpu.VMEM((owners, rows), f32),
            pltpu.VMEM((shards, owners, rows), f32),
            dma((owners,)), dma((chunks,)), dma((1,)),
            dma((shards - 1,)), dma((shards - 1,)),
            dma((1,)), dma((1,)), dma((1,)), dma((1,)), dma((1,)), dma((1,)),
        ],
        compiler_params=pltpu.CompilerParams(
            collective_id=0, has_side_effects=True, vmem_limit_bytes=60 * 1024 * 1024,
            dimension_semantics=("arbitrary",),
        ),
    )(
        hidden_rows[0], norm_gain, norm_bias, target_ids.reshape(1, tokens), ckpt_steps,
        components, unembed[0],
    )

    across = 3 * tile if chunks % 3 == 0 else tile
    out, gram, target = pl.pallas_call(
        mix_kernel,
        grid=(-(-padded // across),),
        in_specs=[pl.BlockSpec((rows, across), lambda j: (0, j)), vmem, vmem, vmem, vmem, vmem],
        out_specs=[pl.BlockSpec((out_rows, across), lambda j: (0, j)), vmem, vmem],
        out_shape=[
            jax.ShapeDtypeStruct((out_rows, width), bf16),
            jax.ShapeDtypeStruct((owners, owners), f32),
            jax.ShapeDtypeStruct((1, tokens), f32),
        ],
        compiler_params=pltpu.CompilerParams(dimension_semantics=("arbitrary",)),
    )(x, whi, wlo, shift, gram, target)
    return out.reshape(COMPONENTS, slab, width), gram, target


def solution(mesh):
    return jax.shard_map(
        functools.partial(per_device, mesh.shape["ckpt"], mesh.shape["vocab"]),
        mesh=mesh,
        in_specs=(
            P("ckpt", None, None),
            P("ckpt", None),
            P("ckpt", None),
            P("ckpt", None, "vocab"),
            P(),
            P(),
            P(),
        ),
        out_specs=(P(None, "ckpt", "vocab"), P(), P("ckpt", None)),
        check_vma=False,
    )
```

```python
import functools

import jax
import jax.numpy as jnp
from jax import lax
from jax.experimental import pallas as pl
from jax.experimental.pallas import tpu as pltpu
from jax.sharding import PartitionSpec as P

COMPONENTS = 8
LANES = 128
HIGH = lax.Precision.HIGHEST
MESH = pl.DeviceIdType.MESH
LOW = -1e30
NT = (((1,), (1,)), ((), ()))


def split_tiles(width):
    tiles = -(-width // LANES)
    best = tiles
    for per in range(1, tiles + 1):
        if tiles % per == 0 and per >= 6:
            best = per
            break
    return best * LANES, tiles // best


def spread_steps(steps_ref, shape, slab):
    lane_owner = lax.broadcasted_iota(jnp.int32, shape, 1) // slab
    out = jnp.zeros(shape, jnp.float32)
    for c in range(steps_ref.shape[0]):
        out = jnp.where(lane_owner == c, steps_ref[c].astype(jnp.float32), out)
    return out


def gather_kernel(
    sizes,
    hidden_ref, gain_ref, bias_ref, ids_ref, steps_ref, comps_ref, w_ref,
    xout_ref, w2_ref, shift_ref, gram_ref, target_ref,
    normed, xsend, xrecv, off, ids, tops, sums, hits, stat, stats, dsend, drecv,
    gsend, grecv, hsend, hrecv,
    send_sem, recv_sem, out_sem, ssend, srecv, dssem, drsem, gssem, grsem, hssem, hrsem,
):
    owners, shards, tokens, width, tile, chunks = sizes
    slab = tokens // owners
    rows = owners * slab
    kinds = COMPONENTS
    me = lax.axis_index("ckpt")
    mine = lax.axis_index("vocab")
    step = pl.program_id(0)
    groups = tile // LANES
    my_rows = pl.ds(pl.multiple_of(me * slab, slab), slab)

    def peer(r):
        return lax.rem(me + r, owners)

    def side(r):
        return lax.rem(mine + r, shards)

    @pl.when(step == 0)
    def _():
        barrier = pltpu.get_barrier_semaphore()
        for r in range(1, owners):
            pl.semaphore_signal(barrier, inc=1, device_id=(peer(r), mine), device_id_type=MESH)
        for r in range(1, shards):
            pl.semaphore_signal(barrier, inc=1, device_id=(me, side(r)), device_id_type=MESH)
        floats = hidden_ref[...].astype(jnp.float32)
        centre = jnp.mean(floats, axis=1, keepdims=True)
        spread = jnp.mean((floats - centre) ** 2, axis=1, keepdims=True)
        normed[...] = (
            (floats - centre) / jnp.sqrt(spread + 1e-05) * gain_ref[...] + bias_ref[...]
        ).astype(jnp.bfloat16)
        wide = jnp.broadcast_to(ids_ref[...].astype(jnp.float32), (LANES, tokens))
        ids[...] = jnp.transpose(wide).astype(jnp.int32)
        tops[...] = jnp.full_like(tops, LOW)
        sums[...] = jnp.zeros_like(sums)
        hits[...] = jnp.zeros_like(hits)

    logits = lax.dot_general(normed[...], w_ref[...], NT, preferred_element_type=jnp.float32)
    first = step * tile
    lane = lax.broadcasted_iota(jnp.int32, (tokens, LANES), 1)

    @pl.when(step == 0)
    def _():
        total = logits[:, :LANES]
        for g in range(1, groups):
            total = total + logits[:, g * LANES:(g + 1) * LANES]
        off[...] = jnp.broadcast_to(
            jnp.sum(total, axis=1, keepdims=True) * (1.0 / tile), off.shape
        )

    shift = off[...]
    for g in range(groups):
        part = logits[:, g * LANES:(g + 1) * LANES]
        inside = (first + g * LANES + lane) < width
        at = pl.multiple_of(first + g * LANES, LANES)
        xsend[:, pl.ds(at, LANES)] = jnp.where(inside, part - shift, 0.0).astype(jnp.bfloat16)

    @pl.when(step == 0)
    def _():
        barrier = pltpu.get_barrier_semaphore()
        pl.semaphore_wait(barrier, owners - 1 + shards - 1)

    def columns(j):
        return pl.ds(pl.multiple_of(j * tile, LANES), tile)

    for r in range(1, owners):
        to = peer(r)
        pltpu.make_async_remote_copy(
            src_ref=xsend.at[pl.ds(pl.multiple_of(to * slab, slab), slab), columns(step)],
            dst_ref=xrecv.at[my_rows, columns(step)],
            send_sem=send_sem.at[r],
            recv_sem=recv_sem.at[step],
            device_id=(to, mine),
            device_id_type=MESH,
        ).start()
    pltpu.make_async_copy(
        xsend.at[my_rows, columns(step)], xrecv.at[my_rows, columns(step)], recv_sem.at[step]
    ).start()

    old_top = tops[...]
    new_top = old_top
    parts = []
    for g in range(groups):
        part = logits[:, g * LANES:(g + 1) * LANES]
        inside = (first + g * LANES + lane) < width
        part = jnp.where(inside, part, LOW)
        parts.append(part)
        new_top = jnp.maximum(new_top, part)
    acc = sums[...] * jnp.exp(old_top - new_top)
    hit = hits[...]
    start = mine * width + first
    wanted = ids[...] - start
    for g in range(groups):
        acc = acc + jnp.exp(parts[g] - new_top)
        col = g * LANES + lane
        hit = hit + jnp.where((col == wanted) & ((first + col) < width), parts[g], 0.0)
    tops[...] = new_top
    sums[...] = acc
    hits[...] = hit

    @pl.when(step == chunks - 1)
    def _():
        top = jnp.max(tops[...], axis=1, keepdims=True)
        total = jnp.sum(sums[...] * jnp.exp(tops[...] - top), axis=1, keepdims=True)
        picked = jnp.sum(hits[...], axis=1, keepdims=True)
        stat[...] = jnp.where(lane == 0, top, jnp.where(lane == 1, total, picked))
        sent = []
        for r in range(1, shards):
            copy = pltpu.make_async_remote_copy(
                src_ref=stat,
                dst_ref=stats.at[r - 1],
                send_sem=ssend.at[r - 1],
                recv_sem=srecv.at[r - 1],
                device_id=(me, side(r)),
                device_id_type=MESH,
            )
            copy.start()
            sent.append(copy)
        for copy in sent:
            copy.wait()
        best = top
        for r in range(shards - 1):
            best = jnp.maximum(best, stats[r][:, 0:1])
        total = total * jnp.exp(top - best)
        for r in range(shards - 1):
            total = total + stats[r][:, 1:2] * jnp.exp(stats[r][:, 0:1] - best)
            picked = picked + stats[r][:, 2:3]
        lse = best + jnp.log(total)
        dsend[...] = jnp.broadcast_to(off[:, 0:1] - lse, dsend.shape)
        dcopies = []
        for r in range(1, owners):
            to = peer(r)
            copy = pltpu.make_async_remote_copy(
                src_ref=dsend.at[pl.ds(pl.multiple_of(to * slab, slab), slab), :],
                dst_ref=drecv.at[my_rows, :],
                send_sem=dssem.at[0],
                recv_sem=drsem.at[0],
                device_id=(to, mine),
                device_id_type=MESH,
            )
            copy.start()
        pltpu.make_async_copy(dsend.at[my_rows, :], drecv.at[my_rows, :], drsem.at[0]).start()
        target_ref[...] = jnp.transpose(
            jnp.broadcast_to(picked - lse, (tokens, LANES))
        )[0:1, :]

        row_k = lax.broadcasted_iota(jnp.int32, (kinds * slab, rows), 0)
        freqs = (row_k // slab + 1).astype(jnp.float32)
        at_steps = spread_steps(steps_ref, (kinds * slab, rows), slab)
        basis = jnp.cos(jnp.pi * freqs * at_steps / 143000.0)
        basis = basis - jnp.mean(basis, axis=1, keepdims=True)
        same = (row_k % slab) == (lax.broadcasted_iota(jnp.int32, (kinds * slab, rows), 1) % slab)
        keep = same & (row_k // slab < comps_ref[0])
        ones = jnp.ones((tile, LANES), jnp.bfloat16)

        def absorb(j, carry):
            products, totals = carry
            block = xrecv.at[:, columns(j)]
            pltpu.make_async_copy(block, block, recv_sem.at[j]).wait()
            pltpu.make_async_copy(block, xout_ref.at[:, columns(j)], out_sem.at[0]).start()
            x = block[...]
            products = products + lax.dot_general(x, x, NT, preferred_element_type=jnp.float32)
            totals = totals + jnp.dot(x, ones, preferred_element_type=jnp.float32)
            return products, totals

        products, totals = lax.fori_loop(
            0, chunks, absorb,
            (jnp.zeros((rows, rows), jnp.float32), jnp.zeros((rows, LANES), jnp.float32)),
        )
        pltpu.make_async_copy(drecv, drecv, drsem.at[0]).wait()
        d = drecv[...].reshape(owners, slab, LANES)
        d = (d - jnp.mean(d, axis=0, keepdims=True)).reshape(rows, LANES)
        lane_r = lax.broadcasted_iota(jnp.int32, (rows, LANES), 1)
        left = jnp.where(lane_r == 0, totals, jnp.where(lane_r == 1, d, 0.0))
        right = jnp.where(
            lane_r == 0, d, jnp.where(lane_r == 1, totals + float(width) * d, 0.0)
        )
        products = products + lax.dot_general(
            left, right, NT, precision=HIGH, preferred_element_type=jnp.float32
        )
        matched = (
            lax.broadcasted_iota(jnp.int32, (rows, rows), 0) % slab
            == lax.broadcasted_iota(jnp.int32, (rows, rows), 1) % slab
        )
        partial = jnp.sum(
            jnp.where(matched, products, 0.0).reshape(owners, slab, rows), axis=1
        )
        gsend[...] = partial
        gcopies = []
        for r in range(1, owners):
            copy = pltpu.make_async_remote_copy(
                src_ref=gsend,
                dst_ref=grecv.at[me],
                send_sem=gssem.at[0],
                recv_sem=grsem.at[0],
                device_id=(peer(r), mine),
                device_id_type=MESH,
            )
            copy.start()
        pltpu.make_async_copy(gsend, grecv.at[me], grsem.at[0]).start()
        pltpu.make_async_copy(grecv, grecv, grsem.at[0]).wait()
        hsend[...] = jnp.sum(grecv[...], axis=0)
        for r in range(1, shards):
            pltpu.make_async_remote_copy(
                src_ref=hsend,
                dst_ref=hrecv.at[mine],
                send_sem=hssem.at[0],
                recv_sem=hrsem.at[0],
                device_id=(me, side(r)),
                device_id_type=MESH,
            ).start()
        pltpu.make_async_copy(hsend, hrecv.at[mine], hrsem.at[0]).start()
        pltpu.make_async_copy(hrecv, hrecv, hrsem.at[0]).wait()
        full = jnp.sum(hrecv[...], axis=0) * (1.0 / (tokens * width * shards))
        full = full - jnp.mean(full, axis=0, keepdims=True)
        own = (
            lax.broadcasted_iota(jnp.int32, (owners, rows), 0)
            == lax.broadcasted_iota(jnp.int32, (owners, rows), 1) // slab
        )
        trace = jnp.sum(
            jnp.sum(jnp.where(own, full, 0.0), axis=1, keepdims=True), axis=0, keepdims=True
        )
        tall = jnp.broadcast_to(full[:, None, :], (owners, slab, rows)).reshape(rows, rows)
        mixed = lax.dot_general(
            basis, tall, NT, precision=HIGH, preferred_element_type=jnp.float32
        )
        mixed = jnp.where(keep, mixed / (trace * (1.0 / owners) + 1e-06) * (1.0 / owners), 0.0)
        high = mixed.astype(jnp.bfloat16)
        half = mixed.shape[0]
        w2_ref[0:half, :] = high
        w2_ref[half:, :] = (mixed - high.astype(jnp.float32)).astype(jnp.bfloat16)
        shift_ref[...] = jnp.dot(mixed, d, precision=HIGH, preferred_element_type=jnp.float32)
        pick = (
            lax.broadcasted_iota(jnp.int32, (rows, LANES), 0) // slab
            == lax.broadcasted_iota(jnp.int32, (rows, LANES), 1)
        ).astype(jnp.float32) - 1.0 / owners
        gram_ref[...] = jnp.dot(
            full, pick, precision=HIGH, preferred_element_type=jnp.float32
        )[:, :owners]

        for r in range(1, owners):
            strip = xsend.at[my_rows, :]
            pltpu.make_async_copy(strip, strip, send_sem.at[r]).wait()
        others = pl.ds(0, rows - slab)
        pltpu.make_async_copy(dsend.at[others, :], dsend.at[others, :], dssem.at[0]).wait()
        less = pl.ds(0, owners - 1)
        pltpu.make_async_copy(grecv.at[less], grecv.at[less], gssem.at[0]).wait()
        fewer = pl.ds(0, shards - 1)
        pltpu.make_async_copy(hrecv.at[fewer], hrecv.at[fewer], hssem.at[0]).wait()
        pltpu.make_async_copy(xrecv, xout_ref, out_sem.at[0]).wait()


def mix_kernel(across, x_ref, w2_ref, shift_ref, gram_in, target_in, out_ref, gram_ref, target_ref):
    start = pl.multiple_of(pl.program_id(0) * across, LANES)
    x = x_ref[:, pl.ds(start, across)]
    both = jnp.dot(w2_ref[...], x, preferred_element_type=jnp.float32)
    half = out_ref.shape[0]
    out_ref[...] = (both[:half] + both[half:] + shift_ref[:, 0:1]).astype(jnp.bfloat16)
    gram_ref[...] = gram_in[...]
    target_ref[...] = target_in[...]


def per_device(owners, shards, hidden_rows, norm_gain, norm_bias, unembed, target_ids, ckpt_steps, components):
    tokens, depth = hidden_rows.shape[1:]
    width = unembed.shape[2]
    slab = tokens // owners
    rows = owners * slab
    out_rows = COMPONENTS * slab
    tile, chunks = split_tiles(width)
    padded = tile * chunks
    sizes = (owners, shards, tokens, width, tile, chunks)
    f32, bf16 = jnp.float32, jnp.bfloat16
    limit = 67043328 - rows * padded * 2 - (5 << 19)
    vmem = pl.BlockSpec(memory_space=pltpu.VMEM)
    smem = pl.BlockSpec(memory_space=pltpu.SMEM)
    dma = pltpu.SemaphoreType.DMA

    x, w2, shift, gram, target = pl.pallas_call(
        functools.partial(gather_kernel, sizes),
        grid=(chunks,),
        in_specs=[
            vmem, vmem, vmem, vmem, smem, smem,
            pl.BlockSpec((tile, depth), lambda j: (j, 0)),
        ],
        out_specs=[pl.BlockSpec(memory_space=pl.ANY), vmem, vmem, vmem, vmem],
        out_shape=[
            jax.ShapeDtypeStruct((rows, padded), bf16),
            jax.ShapeDtypeStruct((2 * out_rows, rows), bf16),
            jax.ShapeDtypeStruct((out_rows, LANES), f32),
            jax.ShapeDtypeStruct((owners, owners), f32),
            jax.ShapeDtypeStruct((1, tokens), f32),
        ],
        scratch_shapes=[
            pltpu.VMEM((tokens, depth), bf16),
            pltpu.VMEM((tokens, padded), bf16),
            pltpu.VMEM((rows, padded), bf16),
            pltpu.VMEM((tokens, LANES), f32),
            pltpu.VMEM((tokens, LANES), jnp.int32),
            pltpu.VMEM((tokens, LANES), f32),
            pltpu.VMEM((tokens, LANES), f32),
            pltpu.VMEM((tokens, LANES), f32),
            pltpu.VMEM((tokens, LANES), f32),
            pltpu.VMEM((shards - 1, tokens, LANES), f32),
            pltpu.VMEM((tokens, LANES), f32),
            pltpu.VMEM((rows, LANES), f32),
            pltpu.VMEM((owners, rows), f32),
            pltpu.VMEM((owners, owners, rows), f32),
            pltpu.VMEM((owners, rows), f32),
            pltpu.VMEM((shards, owners, rows), f32),
            dma((owners,)), dma((chunks,)), dma((1,)),
            dma((shards - 1,)), dma((shards - 1,)),
            dma((1,)), dma((1,)), dma((1,)), dma((1,)), dma((1,)), dma((1,)),
        ],
        compiler_params=pltpu.CompilerParams(
            collective_id=0, has_side_effects=True, vmem_limit_bytes=limit,
            dimension_semantics=("arbitrary",),
        ),
    )(
        hidden_rows[0], norm_gain, norm_bias, target_ids.reshape(1, tokens), ckpt_steps,
        components, unembed[0].T,
    )

    across = -(-(padded // LANES) // 3) * LANES
    out, gram, target = pl.pallas_call(
        functools.partial(mix_kernel, across),
        grid=(padded // across,),
        in_specs=[vmem, vmem, vmem, vmem, vmem],
        out_specs=[pl.BlockSpec((out_rows, across), lambda j: (0, j)), vmem, vmem],
        out_shape=[
            jax.ShapeDtypeStruct((out_rows, width), bf16),
            jax.ShapeDtypeStruct((owners, owners), f32),
            jax.ShapeDtypeStruct((1, tokens), f32),
        ],
        compiler_params=pltpu.CompilerParams(
            dimension_semantics=("arbitrary",),
            vmem_limit_bytes=rows * padded * 2 + 12 * out_rows * across + (6 << 20),
        ),
    )(x, w2, shift, gram, target)
    return out.reshape(COMPONENTS, slab, width), gram, target


def solution(mesh):
    return jax.shard_map(
        functools.partial(per_device, mesh.shape["ckpt"], mesh.shape["vocab"]),
        mesh=mesh,
        in_specs=(
            P("ckpt", None, None),
            P("ckpt", None),
            P("ckpt", None),
            P("ckpt", None, "vocab"),
            P(),
            P(),
            P(),
        ),
        out_specs=(P(None, "ckpt", "vocab"), P(), P("ckpt", None)),
        check_vma=False,
    )
```

```python
import functools

import jax
import jax.numpy as jnp
from jax import lax
from jax.experimental import pallas as pl
from jax.experimental.pallas import tpu as pltpu
from jax.sharding import PartitionSpec as P

COMPONENTS = 8
LANES = 128
HIGH = lax.Precision.HIGHEST
MESH = pl.DeviceIdType.MESH
LOW = -1e30
NT = (((1,), (1,)), ((), ()))


def split_tiles(width):
    tiles = -(-width // LANES)
    best = tiles
    for per in range(1, tiles + 1):
        if tiles % per == 0 and per >= 6:
            best = per
            break
    return best * LANES, tiles // best


def spread_steps(steps_ref, shape):
    lane_owner = lax.broadcasted_iota(jnp.int32, shape, 1) % steps_ref.shape[0]
    out = jnp.zeros(shape, jnp.float32)
    for c in range(steps_ref.shape[0]):
        out = jnp.where(lane_owner == c, steps_ref[c].astype(jnp.float32), out)
    return out


def gather_kernel(
    sizes,
    hidden_hbm, gain_hbm, bias_hbm, ids_hbm, steps_hbm, comps_hbm, w_ref,
    xout_ref, w2_ref, shift_ref, gram_ref, target_ref,
    normed, xsend, xrecv, off, ids, tops, sums, hits, stat, stats, dsend, drecv,
    gsend, grecv,
    hidden_ref, gain_ref, bias_ref, ids_ref, steps_ref, comps_ref, in_sem,
    send_sem, recv_sem, out_sem, ssend, srecv, dssem, drsem, gssem, grsem,
):
    owners, shards, tokens, width, tile, chunks = sizes
    slab = tokens // owners
    rows = owners * slab
    kinds = COMPONENTS
    me = lax.axis_index("ckpt")
    mine = lax.axis_index("vocab")
    step = pl.program_id(0)
    groups = tile // LANES
    my_rows = pl.ds(pl.multiple_of(me * slab, slab), slab)

    def peer(r):
        return lax.rem(me + r, owners)

    def side(r):
        return lax.rem(mine + r, shards)

    @pl.when(step == 0)
    def _():
        loads = []
        for i, (src, dst) in enumerate((
            (hidden_hbm, hidden_ref), (gain_hbm, gain_ref), (bias_hbm, bias_ref),
            (ids_hbm, ids_ref), (steps_hbm, steps_ref), (comps_hbm, comps_ref),
        )):
            load = pltpu.make_async_copy(src, dst, in_sem.at[i])
            load.start()
            loads.append(load)
        barrier = pltpu.get_barrier_semaphore()
        for q in range(shards):
            for r in range(owners):
                if q or r:
                    pl.semaphore_signal(
                        barrier, inc=1, device_id=(peer(r), side(q)), device_id_type=MESH
                    )
        for load in loads:
            load.wait()
        floats = hidden_ref[...].astype(jnp.float32)
        centre = jnp.mean(floats, axis=1, keepdims=True)
        spread = jnp.mean((floats - centre) ** 2, axis=1, keepdims=True)
        normed[...] = (
            (floats - centre) / jnp.sqrt(spread + 1e-05) * gain_ref[...] + bias_ref[...]
        ).astype(jnp.bfloat16)
        wide = jnp.broadcast_to(ids_ref[...].astype(jnp.float32), (LANES, tokens))
        ids[...] = jnp.transpose(wide).astype(jnp.int32)
        tops[...] = jnp.full_like(tops, LOW)
        sums[...] = jnp.zeros_like(sums)
        hits[...] = jnp.zeros_like(hits)

    logits = lax.dot_general(normed[...], w_ref[...], NT, preferred_element_type=jnp.float32)
    first = step * tile
    lane = lax.broadcasted_iota(jnp.int32, (tokens, LANES), 1)

    @pl.when(step == 0)
    def _():
        total = logits[:, :LANES]
        for g in range(1, groups):
            total = total + logits[:, g * LANES:(g + 1) * LANES]
        off[...] = jnp.broadcast_to(
            jnp.sum(total, axis=1, keepdims=True) * (1.0 / tile), off.shape
        )

    shift = off[...]
    for g in range(groups):
        part = logits[:, g * LANES:(g + 1) * LANES]
        inside = (first + g * LANES + lane) < width
        at = pl.multiple_of(first + g * LANES, LANES)
        xsend[:, pl.ds(at, LANES)] = jnp.where(inside, part - shift, 0.0).astype(jnp.bfloat16)

    @pl.when(step == 0)
    def _():
        barrier = pltpu.get_barrier_semaphore()
        pl.semaphore_wait(barrier, owners * shards - 1)

    def columns(j):
        return pl.ds(pl.multiple_of(j * tile, LANES), tile)

    for r in range(1, owners):
        to = peer(r)
        pltpu.make_async_remote_copy(
            src_ref=xsend.at[pl.ds(pl.multiple_of(to * slab, slab), slab), columns(step)],
            dst_ref=xrecv.at[my_rows, columns(step)],
            send_sem=send_sem.at[r],
            recv_sem=recv_sem.at[step],
            device_id=(to, mine),
            device_id_type=MESH,
        ).start()
    pltpu.make_async_copy(
        xsend.at[my_rows, columns(step)], xrecv.at[my_rows, columns(step)], recv_sem.at[step]
    ).start()

    old_top = tops[...]
    new_top = old_top
    parts = []
    for g in range(groups):
        part = logits[:, g * LANES:(g + 1) * LANES]
        inside = (first + g * LANES + lane) < width
        part = jnp.where(inside, part, LOW)
        parts.append(part)
        new_top = jnp.maximum(new_top, part)
    acc = sums[...] * jnp.exp(old_top - new_top)
    hit = hits[...]
    start = mine * width + first
    wanted = ids[...] - start
    for g in range(groups):
        acc = acc + jnp.exp(parts[g] - new_top)
        col = g * LANES + lane
        hit = hit + jnp.where((col == wanted) & ((first + col) < width), parts[g], 0.0)
    tops[...] = new_top
    sums[...] = acc
    hits[...] = hit

    @pl.when(step == chunks - 1)
    def _():
        top = jnp.max(tops[...], axis=1, keepdims=True)
        total = jnp.sum(sums[...] * jnp.exp(tops[...] - top), axis=1, keepdims=True)
        picked = jnp.sum(hits[...], axis=1, keepdims=True)
        stat[...] = jnp.where(lane == 0, top, jnp.where(lane == 1, total, picked))
        sent = []
        for r in range(1, shards):
            copy = pltpu.make_async_remote_copy(
                src_ref=stat,
                dst_ref=stats.at[r - 1],
                send_sem=ssend.at[r - 1],
                recv_sem=srecv.at[r - 1],
                device_id=(me, side(r)),
                device_id_type=MESH,
            )
            copy.start()
            sent.append(copy)
        for copy in sent:
            copy.wait()
        best = top
        for r in range(shards - 1):
            best = jnp.maximum(best, stats[r][:, 0:1])
        total = total * jnp.exp(top - best)
        for r in range(shards - 1):
            total = total + stats[r][:, 1:2] * jnp.exp(stats[r][:, 0:1] - best)
            picked = picked + stats[r][:, 2:3]
        lse = best + jnp.log(total)
        dsend[...] = jnp.broadcast_to(off[:, 0:1] - lse, dsend.shape)
        dcopies = []
        for r in range(1, owners):
            to = peer(r)
            copy = pltpu.make_async_remote_copy(
                src_ref=dsend.at[pl.ds(pl.multiple_of(to * slab, slab), slab), :],
                dst_ref=drecv.at[my_rows, :],
                send_sem=dssem.at[0],
                recv_sem=drsem.at[0],
                device_id=(to, mine),
                device_id_type=MESH,
            )
            copy.start()
        pltpu.make_async_copy(dsend.at[my_rows, :], drecv.at[my_rows, :], drsem.at[0]).start()
        target_ref[...] = jnp.transpose(
            jnp.broadcast_to(picked - lse, (tokens, LANES))
        )[0:1, :]

        flats = max(owners * owners, LANES)

        def iota(shape, axis):
            return lax.broadcasted_iota(jnp.int32, shape, axis)

        slot = mine * owners + me
        flat_lane = iota((owners, flats), 1)
        flat_own = flat_lane // owners == iota((owners, flats), 0)
        flat_diag = iota((1, flats), 1) // owners == iota((1, flats), 1) % owners
        to_flat = (iota((rows, flats), 0) // slab == iota((rows, flats), 1) % owners).astype(
            jnp.float32
        )
        from_flat = (iota((flats, rows), 0) // owners == iota((flats, rows), 1) // slab).astype(
            jnp.float32
        )
        flat_pick = (iota((flats, LANES), 0) % owners == iota((flats, LANES), 1)).astype(
            jnp.float32
        ) - 1.0 / owners
        row_k = iota((kinds * slab, flats), 0) // slab
        at_steps = spread_steps(steps_ref, (kinds * slab, flats))
        basis = jnp.cos(jnp.pi * (row_k + 1).astype(jnp.float32) * at_steps / 143000.0)
        flat_basis = basis - jnp.mean(basis, axis=1, keepdims=True)
        row_r = iota((kinds * slab, rows), 0)
        same = (row_r % slab) == (iota((kinds * slab, rows), 1) % slab)
        keep = same & (row_r // slab < comps_ref[0])
        ones = jnp.ones((tile, LANES), jnp.bfloat16)

        def absorb(j, carry):
            products, totals = carry
            block = xrecv.at[:, columns(j)]
            pltpu.make_async_copy(block, block, recv_sem.at[j]).wait()
            pltpu.make_async_copy(block, xout_ref.at[:, columns(j)], out_sem.at[0]).start()
            x = block[...]
            products = products + lax.dot_general(x, x, NT, preferred_element_type=jnp.float32)
            totals = totals + jnp.dot(x, ones, preferred_element_type=jnp.float32)
            return products, totals

        products, totals = lax.fori_loop(
            0, chunks, absorb,
            (jnp.zeros((rows, rows), jnp.float32), jnp.zeros((rows, LANES), jnp.float32)),
        )
        pltpu.make_async_copy(drecv, drecv, drsem.at[0]).wait()
        d = drecv[...].reshape(owners, slab, LANES)
        d = (d - jnp.mean(d, axis=0, keepdims=True)).reshape(rows, LANES)
        d_row = jnp.transpose(d)[0:1, :]
        lane_r = lax.broadcasted_iota(jnp.int32, (rows, LANES), 1)
        left = jnp.where(lane_r == 0, totals, jnp.where(lane_r == 1, d, 0.0))
        right = jnp.where(
            lane_r == 0, d, jnp.where(lane_r == 1, totals + float(width) * d, 0.0)
        )
        products = products + lax.dot_general(
            left, right, NT, precision=HIGH, preferred_element_type=jnp.float32
        )
        matched = (
            lax.broadcasted_iota(jnp.int32, (rows, rows), 0) % slab
            == lax.broadcasted_iota(jnp.int32, (rows, rows), 1) % slab
        )
        partial = jnp.sum(
            jnp.where(matched, products, 0.0).reshape(owners, slab, rows), axis=1
        )
        partial = partial - jnp.mean(partial, axis=0, keepdims=True)
        spreadout = jnp.dot(partial, to_flat, precision=HIGH, preferred_element_type=jnp.float32)
        gsend[...] = jnp.sum(jnp.where(flat_own, spreadout, 0.0), axis=0, keepdims=True)
        for q in range(shards):
            for r in range(owners):
                if q or r:
                    pltpu.make_async_remote_copy(
                        src_ref=gsend,
                        dst_ref=grecv.at[slot],
                        send_sem=gssem.at[0],
                        recv_sem=grsem.at[0],
                        device_id=(peer(r), side(q)),
                        device_id_type=MESH,
                    ).start()
        pltpu.make_async_copy(gsend, grecv.at[slot], grsem.at[0]).start()
        pltpu.make_async_copy(grecv, grecv, grsem.at[0]).wait()
        flat = jnp.sum(grecv[...], axis=0) * (1.0 / (tokens * width * shards))
        trace = jnp.sum(jnp.where(flat_diag, flat, 0.0), axis=1, keepdims=True)
        mixed = jnp.dot(
            flat_basis * flat, from_flat, precision=HIGH, preferred_element_type=jnp.float32
        )
        mixed = jnp.where(keep, mixed / (trace * (1.0 / owners) + 1e-06) * (1.0 / owners), 0.0)
        high = mixed.astype(jnp.bfloat16)
        half = mixed.shape[0]
        w2_ref[0:half, :] = high
        w2_ref[half:, :] = (mixed - high.astype(jnp.float32)).astype(jnp.bfloat16)
        shift_ref[...] = jnp.broadcast_to(
            jnp.sum(mixed * d_row, axis=1, keepdims=True), shift_ref.shape
        )
        gram_ref[...] = jnp.dot(
            jnp.where(flat_own, flat, 0.0), flat_pick, precision=HIGH,
            preferred_element_type=jnp.float32,
        )[:, :owners]

        for r in range(1, owners):
            strip = xsend.at[my_rows, :]
            pltpu.make_async_copy(strip, strip, send_sem.at[r]).wait()
        others = pl.ds(0, rows - slab)
        pltpu.make_async_copy(dsend.at[others, :], dsend.at[others, :], dssem.at[0]).wait()
        less = pl.ds(0, owners * shards - 1)
        pltpu.make_async_copy(grecv.at[less], grecv.at[less], gssem.at[0]).wait()
        pltpu.make_async_copy(xrecv, xout_ref, out_sem.at[0]).wait()


def mix_kernel(across, x_ref, w2_ref, shift_ref, gram_in, target_in, out_ref, gram_ref, target_ref):
    start = pl.multiple_of(pl.program_id(0) * across, LANES)
    x = x_ref[:, pl.ds(start, across)]
    both = jnp.dot(w2_ref[...], x, preferred_element_type=jnp.float32)
    half = out_ref.shape[0]
    out_ref[...] = (both[:half] + both[half:] + shift_ref[:, 0:1]).astype(jnp.bfloat16)
    gram_ref[...] = gram_in[...]
    target_ref[...] = target_in[...]


def per_device(owners, shards, hidden_rows, norm_gain, norm_bias, unembed, target_ids, ckpt_steps, components):
    tokens, depth = hidden_rows.shape[1:]
    width = unembed.shape[2]
    slab = tokens // owners
    rows = owners * slab
    out_rows = COMPONENTS * slab
    tile, chunks = split_tiles(width)
    padded = tile * chunks
    sizes = (owners, shards, tokens, width, tile, chunks)
    f32, bf16 = jnp.float32, jnp.bfloat16
    limit = 67043328 - min(depth * width * 2 - (1 << 20), 16 << 20)
    vmem = pl.BlockSpec(memory_space=pltpu.VMEM)
    hbm = pl.BlockSpec(memory_space=pltpu.HBM)
    dma = pltpu.SemaphoreType.DMA

    x, w2, shift, gram, target = pl.pallas_call(
        functools.partial(gather_kernel, sizes),
        grid=(chunks,),
        in_specs=[
            hbm, hbm, hbm, hbm, hbm, hbm,
            pl.BlockSpec((tile, depth), lambda j: (j, 0)),
        ],
        out_specs=[pl.BlockSpec(memory_space=pl.ANY), vmem, vmem, vmem, vmem],
        out_shape=[
            jax.ShapeDtypeStruct((rows, padded), bf16),
            jax.ShapeDtypeStruct((2 * out_rows, rows), bf16),
            jax.ShapeDtypeStruct((out_rows, LANES), f32),
            jax.ShapeDtypeStruct((owners, owners), f32),
            jax.ShapeDtypeStruct((1, tokens), f32),
        ],
        scratch_shapes=[
            pltpu.VMEM((tokens, depth), bf16),
            pltpu.VMEM((tokens, padded), bf16),
            pltpu.VMEM((rows, padded), bf16),
            pltpu.VMEM((tokens, LANES), f32),
            pltpu.VMEM((tokens, LANES), jnp.int32),
            pltpu.VMEM((tokens, LANES), f32),
            pltpu.VMEM((tokens, LANES), f32),
            pltpu.VMEM((tokens, LANES), f32),
            pltpu.VMEM((tokens, LANES), f32),
            pltpu.VMEM((shards - 1, tokens, LANES), f32),
            pltpu.VMEM((tokens, LANES), f32),
            pltpu.VMEM((rows, LANES), f32),
            pltpu.VMEM((1, max(owners * owners, LANES)), f32),
            pltpu.VMEM((owners * shards, 1, max(owners * owners, LANES)), f32),
            pltpu.VMEM((tokens, depth), bf16),
            pltpu.VMEM((1, depth), f32),
            pltpu.VMEM((1, depth), f32),
            pltpu.VMEM((1, tokens), jnp.int32),
            pltpu.SMEM((owners,), jnp.int32),
            pltpu.SMEM((1,), jnp.int32),
            dma((6,)),
            dma((owners,)), dma((chunks,)), dma((1,)),
            dma((shards - 1,)), dma((shards - 1,)),
            dma((1,)), dma((1,)), dma((1,)), dma((1,)),
        ],
        compiler_params=pltpu.CompilerParams(
            collective_id=0, has_side_effects=True, vmem_limit_bytes=limit,
            dimension_semantics=("arbitrary",),
        ),
    )(*(
        pltpu.with_memory_space_constraint(a, pltpu.HBM) for a in (
            hidden_rows[0], norm_gain, norm_bias, target_ids.reshape(1, tokens), ckpt_steps,
        )
    ), components, unembed[0].T)

    across = -(-(padded // LANES) // 3) * LANES
    out, gram, target = pl.pallas_call(
        functools.partial(mix_kernel, across),
        grid=(padded // across,),
        in_specs=[vmem, vmem, vmem, vmem, vmem],
        out_specs=[pl.BlockSpec((out_rows, across), lambda j: (0, j)), vmem, vmem],
        out_shape=[
            jax.ShapeDtypeStruct((out_rows, width), bf16),
            jax.ShapeDtypeStruct((owners, owners), f32),
            jax.ShapeDtypeStruct((1, tokens), f32),
        ],
        compiler_params=pltpu.CompilerParams(
            dimension_semantics=("arbitrary",),
            vmem_limit_bytes=rows * padded * 2 + 12 * out_rows * across + (6 << 20),
        ),
    )(x, w2, shift, gram, target)
    return out.reshape(COMPONENTS, slab, width), gram, target


def solution(mesh):
    return jax.shard_map(
        functools.partial(per_device, mesh.shape["ckpt"], mesh.shape["vocab"]),
        mesh=mesh,
        in_specs=(
            P("ckpt", None, None),
            P("ckpt", None),
            P("ckpt", None),
            P("ckpt", None, "vocab"),
            P(),
            P(),
            P(),
        ),
        out_specs=(P(None, "ckpt", "vocab"), P(), P("ckpt", None)),
        check_vma=False,
    )
```
